128 devices in a mesh: row: 8 (over y, core), col: 16 (over x, z).
Axes of the slice: x: 4, y: 4, z: 4, core: 2. Of those that a mesh axis runs over, the one named last changes fastest.
Arguments:
- b_tensor: bfloat16 [128, 1024, 1024], P('col', 'row'), may hold values from -6 to 6
- occ_green: bfloat16 [1024, 1024], P(('row', 'col')), may hold values from -0.1875 to 0.1875
- virt_green: bfloat16 [1024, 1024], P(('row', 'col')), may hold values from -0.1875 to 0.1875
- b_mask: int32 [1, 8, 8], replicated, may hold values 0 or 1
- occ_mask: int32 [8, 8], replicated, may hold values 0 or 1
- virt_mask: int32 [8, 8], replicated, may hold values 0 or 1
Outputs:
- chi: float32 [128, 128], P(('row', 'col'))
The draws below stay inside these ranges and needn't reach their ends.
All inputs are finite; a program needn't handle non-finite values.
Results may differ from the reference program's by a relative error of at most 0.0041.
Values may be sent and summed in bfloat16 or wider, within the bound.
A program may use at most 64 MiB of HBM per device.

```python
import jax
import jax.numpy as jnp
from jax import lax

TILE = 128
AO_TILES = 8
RI_TILES = 1
NAO = 1024
NP = 128


def touch_ends(array, stream_key, low, largest):
    spot = [jax.random.randint(jax.random.fold_in(stream_key, axis), (), 0, length) for axis, length in enumerate(array.shape)]
    longest = array.shape.index(max(array.shape))
    neighbour = spot[:longest] + [(spot[longest] + 1) % array.shape[longest]] + spot[longest + 1:]
    return array.at[tuple(spot)].set(low).at[tuple(neighbour)].set(largest)


def steps_of(stream_key, extent, split, least, top_value):
    def one(axis_at, parts):
        steps = jax.random.uniform(jax.random.fold_in(jax.random.fold_in(stream_key, 6), axis_at), (parts,), jnp.float32, least / len(split), top_value / len(split))
        return jnp.repeat(jnp.exp(steps), extent[axis_at] // parts).reshape((-1,) + (1,) * (len(extent) - axis_at - 1))

    loudness = one(*split[0])
    for cut in split[1:]:
        loudness = loudness * one(*cut)
    return loudness


def centred(rng, dims, scale, reach, split=(), dtype=jnp.bfloat16):
    result = jax.random.normal(rng, dims, jnp.float32) * scale
    if len(split) > 0:
        result = steps_of(rng, dims, split, -0.22, 0.18) * result
    return jnp.clip(result, min=-reach, max=reach).astype(dtype)


def setup_inputs(seed: int = 0) -> dict:
    streams_of = jax.random.split(jax.random.key(seed), 7)
    b_tensor = centred(streams_of[0], (NP, NAO, NAO), 1.0, 6.0, ((0, 16), (1, 8)))
    occ_green = centred(streams_of[1], (NAO, NAO), NAO ** -0.5, 0.1875, ((0, 128),))
    virt_green = centred(streams_of[2], (NAO, NAO), NAO ** -0.5, 0.1875, ((0, 128),))
    b_mask = touch_ends((jax.random.randint(streams_of[3], (RI_TILES, AO_TILES, AO_TILES), 0, 4) < 3).astype(jnp.int32), jax.random.fold_in(streams_of[3], 1), 0, 1)
    occ_mask = touch_ends((jax.random.randint(streams_of[4], (AO_TILES, AO_TILES), 0, 4) < 3).astype(jnp.int32), jax.random.fold_in(streams_of[4], 1), 0, 1)
    virt_mask = touch_ends((jax.random.randint(streams_of[5], (AO_TILES, AO_TILES), 0, 4) < 3).astype(jnp.int32), jax.random.fold_in(streams_of[5], 1), 0, 1)
    return dict(b_tensor=b_tensor, occ_green=occ_green, virt_green=virt_green, b_mask=b_mask, occ_mask=occ_mask, virt_mask=virt_mask)


def expand_pair(mask):
    return jnp.repeat(jnp.repeat(mask, TILE, axis=0), TILE, axis=1).astype(jnp.bfloat16)


def reference(b_tensor, occ_green, virt_green, b_mask, occ_mask, virt_mask):
    occ = occ_green * expand_pair(occ_mask)
    virt = virt_green * expand_pair(virt_mask)
    blocks = b_tensor.reshape(RI_TILES, TILE, NAO, NAO)

    def one_tile(items):
        block, mask = items
        masked = block * expand_pair(mask)[None]
        half = jnp.dot(masked.reshape(-1, NAO), virt, preferred_element_type=jnp.float32)
        half = half.astype(jnp.bfloat16).reshape(TILE, NAO, NAO)
        full = jnp.einsum("lm,pms->pls", occ.astype(jnp.float32), half.astype(jnp.float32))
        return full.astype(jnp.bfloat16), masked

    full_all, masked_all = lax.map(one_tile, (blocks, b_mask))
    total = jnp.dot(full_all.reshape(NP, -1), masked_all.reshape(NP, -1).T, preferred_element_type=jnp.float32)
    return total * (-2.0 / NAO)
```

```python
import functools

import jax
import jax.numpy as jnp
from jax import lax
from jax.experimental import pallas as pl
from jax.experimental.pallas import tpu as pltpu
from jax.sharding import PartitionSpec as P

TILE = 128
ROWS, COLS = 8, 16
DEVICES = ROWS * COLS
N = 1024
NP = 128
SUB = 8
F32, BF16 = jnp.float32, jnp.bfloat16


def to(row, col):
    return {"row": row, "col": col}


def send(src, dst, send_sem, recv_sem, row, col):
    pltpu.make_async_remote_copy(
        src_ref=src,
        dst_ref=dst,
        send_sem=send_sem,
        recv_sem=recv_sem,
        device_id=to(row, col),
        device_id_type=pl.DeviceIdType.MESH,
    ).start()


def wait(ref, sem):
    pltpu.make_async_copy(ref, ref, sem).wait()


def flat(pieces):
    return pieces.astype(F32).reshape(-1, pieces.shape[-1])


def lanes(mask_ref, *index):
    return jnp.concatenate(
        [jnp.full((1, TILE), mask_ref[(*index, j)].astype(F32)) for j in range(N // TILE)], axis=1
    )


def kernel(
    b_ref,
    occ_ref,
    virt_ref,
    b_mask,
    occ_mask,
    virt_mask,
    out_ref,
    gath,
    bp,
    bk,
    virt,
    occ,
    half,
    full,
    full_k,
    w,
    part,
    part_in,
    line,
    line_in,
    local_sem,
    ag_send,
    ag_recv,
    row_send,
    row_recv,
    col_send,
    col_recv,
    full_send,
    full_recv,
    red_send,
    red_recv,
):
    r, c = lax.axis_index("row"), lax.axis_index("col")
    y, k = r // 2, r % 2
    x, z = c // 4, c % 4
    me = r * COLS + c

    mate = r + 1 - 2 * k

    @pl.when(k == 0)
    def _():
        gath[0, r, x, z] = virt_ref[...]
        send(occ_ref, gath.at[1, r, x, z], ag_send.at[0], ag_recv.at[0], mate, c)

    @pl.when(k == 1)
    def _():
        gath[1, r, x, z] = occ_ref[...]
        send(virt_ref, gath.at[0, r, x, z], ag_send.at[0], ag_recv.at[0], mate, c)

    own_b = pltpu.make_async_copy(b_ref.at[r], bp.at[r], row_recv.at[0])
    own_b.start()

    @pl.loop(1, ROWS)
    def _(i):
        to_row = (r + i) % ROWS
        send(b_ref.at[to_row], bp.at[r], row_send, row_recv.at[i], to_row, c)

    wait(gath.at[0, 0, 0, 0], ag_recv.at[0])
    for i in range(1, 4):
        mine = gath.at[k, pl.ds(2 * y, 2), x, z]
        send(mine, mine, ag_send.at[1], ag_recv.at[1], 2 * ((y + i) % 4) + k, c)
    wait(gath.at[0, pl.ds(0, 6), 0, 0], ag_recv.at[1])
    mine2 = gath.at[k, :, x, z]
    for i in range(1, 4):
        to_col = jnp.where(k == 0, (x + i) % 4 * 4 + z, x * 4 + (z + i) % 4)
        send(mine2, mine2, ag_send.at[2], ag_recv.at[2], r, to_col)
    wait(gath.at[0, :, pl.ds(0, 3), 0], ag_recv.at[2])

    @pl.when(k == 0)
    def _():
        mine3 = gath.at[0, :, :, z]
        for i in range(1, 4):
            send(mine3, mine3, ag_send.at[3], ag_recv.at[3], r, x * 4 + (z + i) % 4)

    @pl.when(k == 1)
    def _():
        mine3 = gath.at[1, :, x]
        for i in range(1, 4):
            send(mine3, mine3, ag_send.at[3], ag_recv.at[3], r, (x + i) % 4 * 4 + z)

    wait(gath.at[0, :, pl.ds(0, 3)], ag_recv.at[3])
    send(gath.at[k], gath.at[k], ag_send.at[4], ag_recv.at[4], mate, c)

    own_k = pltpu.make_async_copy(b_ref.at[:, c], bk.at[pl.ds(c * 8, 8)], col_recv)
    own_k.start()

    @pl.loop(1, COLS)
    def _(j):
        to_col = (c + j) % COLS
        send(b_ref.at[:, to_col], bk.at[pl.ds(c * 8, 8)], col_send, col_recv, r, to_col)

    wait(gath.at[0], ag_recv.at[4])

    @pl.loop(0, ROWS)
    def _(i):
        rows = pl.ds(i * TILE, TILE)
        virt[rows, :] = (flat(gath[0, i].reshape(COLS, SUB, N)) * lanes(virt_mask, i)).astype(BF16)
        occ[rows, :] = (flat(gath[1, i].reshape(COLS, SUB, N)) * lanes(occ_mask, i)).astype(BF16)

    @pl.loop(0, ROWS)
    def _(i):
        src = (r + ROWS - i) % ROWS
        wait(bp.at[0], row_recv.at[i])
        masked = (flat(bp[src]) * lanes(b_mask, 0, src)).astype(BF16)
        rows = pl.ds(pl.multiple_of(src * TILE, TILE), TILE)
        half[rows, :] = jnp.dot(masked, virt[...], preferred_element_type=F32).astype(BF16)

    slot = ((c % 2) * 8 + r) * 8 + c // 2

    @pl.loop(0, ROWS)
    def _(i):
        block = (r + i) % ROWS
        rows = pl.ds(pl.multiple_of(block * TILE, TILE), TILE)
        done = jnp.dot(occ[rows, :], half[...], preferred_element_type=F32)
        done = done * lanes(b_mask, 0, block)
        full[pl.ds(block * COLS, COLS)] = done.reshape(COLS, SUB, N).astype(BF16)

        @pl.loop(0, COLS)
        def _(j):
            to_col = (c + j) % COLS
            piece = full.at[block * COLS + to_col]

            @pl.when(i + j > 0)
            def _():
                send(piece, full_k.at[slot], full_send, full_recv, block, to_col)

            @pl.when(i + j == 0)
            def _():
                pltpu.make_async_copy(piece, full_k.at[slot], full_recv).start()

    row_id = lax.broadcasted_iota(jnp.int32, (SUB, N), 0)
    col_id = lax.broadcasted_iota(jnp.int32, (SUB, N), 1)
    same = (row_id == col_id % SUB)[None]
    wait(bk, col_recv)
    wait(full_k, full_recv)
    right = flat(bk[...]).astype(BF16)
    for i in range(4):
        left = flat(full_k[pl.ds(i * 32, 32)]).astype(BF16)
        cross = lax.dot_general(left, right, (((1,), (1,)), ((), ())), preferred_element_type=F32)
        w[pl.ds(i * 32, 32), :] = jnp.sum(jnp.where(same, cross.reshape(32, SUB, N), 0.0), axis=1)
    pick = lax.broadcasted_iota(jnp.int32, (N, NP), 0) // SUB
    pick = (pick == lax.broadcasted_iota(jnp.int32, (N, NP), 1)).astype(F32)
    sums = jnp.dot(w[...], pick, preferred_element_type=F32, precision=lax.Precision.HIGHEST)
    part[...] = sums.reshape(COLS, ROWS, NP)

    own_part = pltpu.make_async_copy(part.at[c], part_in.at[c], red_recv.at[0])
    own_part.start()

    @pl.loop(1, COLS)
    def _(j):
        to_col = (c + j) % COLS
        send(part.at[to_col], part_in.at[c], red_send.at[0], red_recv.at[0], r, to_col)

    wait(part_in, red_recv.at[0])
    line[...] = jnp.sum(part_in[...], axis=0).reshape(ROWS, 1, NP)
    own_line = pltpu.make_async_copy(line.at[r], line_in.at[r], red_recv.at[1])
    own_line.start()

    @pl.loop(1, ROWS)
    def _(i):
        to_row = (r + i) % ROWS
        send(line.at[to_row], line_in.at[r], red_send.at[1], red_recv.at[1], to_row, c)

    wait(line_in, red_recv.at[1])
    out_ref[...] = jnp.sum(line_in[...], axis=0) * (-2.0 / N)

    wait(gath.at[0, 0, 0, 0], ag_send.at[0])
    wait(gath.at[0, pl.ds(0, 6), 0, 0], ag_send.at[1])
    wait(gath.at[0, :, pl.ds(0, 3), 0], ag_send.at[2])
    wait(gath.at[0, :, pl.ds(0, 3)], ag_send.at[3])
    wait(gath.at[0], ag_send.at[4])
    wait(bp.at[pl.ds(0, ROWS - 1)], row_send)
    wait(bk.at[pl.ds(0, 8 * (COLS - 1))], col_send)
    wait(full_k.at[pl.ds(0, DEVICES - 1)], full_send)
    wait(part_in.at[pl.ds(0, COLS - 1)], red_send.at[0])
    wait(line_in.at[pl.ds(0, ROWS - 1)], red_send.at[1])


def per_device(b_tensor, occ_green, virt_green, b_mask, occ_mask, virt_mask):
    vmem = pl.BlockSpec(memory_space=pltpu.VMEM)
    smem = pl.BlockSpec(memory_space=pltpu.SMEM)
    dma = pltpu.SemaphoreType.DMA
    return pl.pallas_call(
        kernel,
        out_shape=jax.ShapeDtypeStruct((1, NP), F32),
        in_specs=[pl.BlockSpec(memory_space=pl.ANY), vmem, vmem, smem, smem, smem],
        out_specs=vmem,
        scratch_shapes=[
            pltpu.VMEM((2, ROWS, 4, 4, SUB, N), BF16),
            pltpu.VMEM((ROWS, COLS, SUB, N), BF16),
            pltpu.VMEM((NP, SUB, N), BF16),
            pltpu.VMEM((N, N), BF16),
            pltpu.VMEM((N, N), BF16),
            pltpu.VMEM((N, N), BF16),
            pltpu.VMEM((DEVICES, SUB, N), BF16),
            pltpu.VMEM((NP, SUB, N), BF16),
            pltpu.VMEM((NP, N), F32),
            pltpu.VMEM((COLS, ROWS, NP), F32),
            pltpu.VMEM((COLS, ROWS, NP), F32),
            pltpu.VMEM((ROWS, 1, NP), F32),
            pltpu.VMEM((ROWS, 1, NP), F32),
            dma,
            dma((5,)),
            dma((5,)),
            dma,
            dma((ROWS,)),
            dma,
            dma,
            dma,
            dma,
            dma((2,)),
            dma((2,)),
        ],
        compiler_params=pltpu.CompilerParams(
            has_side_effects=True, vmem_limit_bytes=48 * 1024 * 1024
        ),
        name="chi",
    )(b_tensor.reshape(8, COLS, SUB, N), occ_green, virt_green, b_mask, occ_mask, virt_mask)


def solution(mesh):
    return jax.shard_map(
        per_device,
        mesh=mesh,
        in_specs=(
            P("col", "row", None),
            P(("row", "col"), None),
            P(("row", "col"), None),
            P(),
            P(),
            P(),
        ),
        out_specs=P(("row", "col"), None),
        check_vma=False,
    )
```

```python
import jax
import jax.numpy as jnp
from jax import lax
from jax.experimental import pallas as pl
from jax.experimental.pallas import tpu as pltpu
from jax.sharding import PartitionSpec as P

TILE = 128
ROWS, COLS = 8, 16
DEVICES = ROWS * COLS
N = 1024
NP = 128
SUB = 8
GROUPS = 4
F32, BF16 = jnp.float32, jnp.bfloat16


def send(src, dst, send_sem, recv_sem, row, col):
    pltpu.make_async_remote_copy(
        src_ref=src,
        dst_ref=dst,
        send_sem=send_sem,
        recv_sem=recv_sem,
        device_id={"row": row, "col": col},
        device_id_type=pl.DeviceIdType.MESH,
    ).start()


def greet(sem, row, col):
    pl.semaphore_signal(
        sem, inc=1, device_id={"row": row, "col": col}, device_id_type=pl.DeviceIdType.MESH
    )


def wait(ref, sem):
    pltpu.make_async_copy(ref, ref, sem).wait()


def flat(pieces):
    return pieces.astype(F32).reshape(-1, N).astype(BF16)


def lanes(mask_ref, row):
    return jnp.concatenate(
        [jnp.full((1, TILE), mask_ref[row, j].astype(F32)) for j in range(N // TILE)], axis=1
    )


def kernel(
    b_hbm,
    occ_hbm,
    virt_hbm,
    b_mask_hbm,
    occ_mask_hbm,
    virt_mask_hbm,
    out_ref,
    b_mask,
    occ_mask,
    virt_mask,
    b,
    own,
    gath,
    bp,
    bk,
    virt,
    half,
    full,
    full_k,
    right,
    part,
    part_in,
    in_sem,
    b_sem,
    ag_send,
    ag_recv,
    mate_send,
    mate_recv,
    row_send,
    row_recv,
    col_send,
    col_recv,
    full_send,
    full_recv,
    red_send,
    red_recv,
):
    r, c = lax.axis_index("row"), lax.axis_index("col")
    y, k = r // 2, r % 2
    x, z = c // 4, c % 4
    me = r * COLS + c
    mate = r + 1 - 2 * k

    loads = [
        pltpu.make_async_copy(b_mask_hbm.at[0], b_mask, in_sem.at[0]),
        pltpu.make_async_copy(occ_mask_hbm, occ_mask, in_sem.at[1]),
        pltpu.make_async_copy(virt_mask_hbm, virt_mask, in_sem.at[2]),
        pltpu.make_async_copy(virt_hbm, own.at[0], in_sem.at[3]),
        pltpu.make_async_copy(occ_hbm, own.at[1], in_sem.at[4]),
    ]
    for load in loads:
        load.start()
    for p in range(8):
        pltpu.make_async_copy(b_hbm.at[p], b.at[p], b_sem.at[p]).start()

    barrier = pltpu.get_barrier_semaphore()
    for i in range(1, ROWS):
        greet(barrier, (r + i) % ROWS, c)
    for i in range(1, 4):
        greet(barrier, r, (x + i) % 4 * 4 + z)
        greet(barrier, r, x * 4 + (z + i) % 4)

    for load in loads:
        load.wait()
    own[0] = (own[0].astype(F32) * lanes(virt_mask, r)).astype(BF16)
    own[1] = (own[1].astype(F32) * lanes(occ_mask, r)).astype(BF16)
    keep = lanes(b_mask, r)[None]

    @pl.loop(0, 8)
    def _(p):
        wait(b.at[0], b_sem.at[p])
        b[p] = (b[p].astype(F32) * keep).astype(BF16)

    pl.semaphore_wait(barrier, ROWS - 1 + 6)

    for dk in range(2):
        to_k = (k + dk) % 2
        for dy in (0, 1, 3, 2):
            to_y = (y + dy) % 4
            if dy + dk:
                send(
                    own.at[to_k],
                    gath.at[to_k, y, k, x, z],
                    ag_send.at[0],
                    ag_recv.at[0],
                    to_y * 2 + to_k,
                    c,
                )
            else:
                pltpu.make_async_copy(own.at[k], gath.at[k, y, k, x, z], ag_recv.at[0]).start()

    for dk in range(2):
        for dy in (0, 1, 3, 2):
            to_row = (y + dy) % 4 * 2 + (k + dk) % 2
            if dy + dk:
                send(b.at[to_row], bp.at[r], row_send, row_recv.at[dy], to_row, c)
            else:
                pltpu.make_async_copy(b.at[r], bp.at[r], row_recv.at[0]).start()

    def by_columns(dx, dz):
        to_col = (x + dx) % 4 * 4 + (z + dz) % 4
        send(b.at[:, to_col], bk.at[pl.ds(c * 8, 8)], col_send, col_recv, r, to_col)

    pltpu.make_async_copy(b.at[:, c], bk.at[pl.ds(c * 8, 8)], col_recv).start()
    for i in (1, 3, 2):
        by_columns(0, i)
        by_columns(i, 0)

    wait(gath.at[0, :, :, 0, 0], ag_recv.at[0])
    line = gath.at[k, :, :, x, z]
    for i in (1, 3, 2):
        to_col = jnp.where(k == 0, (x + i) % 4 * 4 + z, x * 4 + (z + i) % 4)
        send(line, line, ag_send.at[1], ag_recv.at[1], r, to_col)
    wait(gath.at[0, :, :, pl.ds(0, 3), 0], ag_recv.at[1])

    @pl.when(k == 0)
    def _():
        plane = gath.at[0, :, :, :, z]
        for i in (1, 3, 2):
            send(plane, plane, ag_send.at[2], ag_recv.at[1 + i], r, x * 4 + (z + i) % 4)
        send(plane, plane, mate_send, mate_recv, mate, c)
        for i in (1, 3, 2):
            plane = gath.at[0, :, :, :, (z + 4 - i) % 4]
            wait(plane, ag_recv.at[1 + i])
            send(plane, plane, mate_send, mate_recv, mate, c)

    @pl.when(k == 1)
    def _():
        plane = gath.at[1, :, :, x]
        for i in (1, 3, 2):
            send(plane, plane, ag_send.at[2], ag_recv.at[1 + i], r, (x + i) % 4 * 4 + z)
        send(plane, plane, mate_send, mate_recv, mate, c)
        for i in (1, 3, 2):
            plane = gath.at[1, :, :, (x + 4 - i) % 4]
            wait(plane, ag_recv.at[1 + i])
            send(plane, plane, mate_send, mate_recv, mate, c)

    for u in range(4):
        for t in range(1, 4):
            if (t + u) % 4:
                by_columns(t, (t + u) % 4)

    wait(gath.at[0], mate_recv)

    for row in range(ROWS):
        virt[pl.ds(row * TILE, TILE), :] = flat(gath[0, row // 2, row % 2])
    for dy in (0, 1, 3, 2):
        from_y = (y + 4 - dy) % 4
        wait(bp.at[pl.ds(0, 2)], row_recv.at[dy])
        rows = pl.ds(pl.multiple_of(from_y * 256, 256), 256)
        block = flat(bp[pl.ds(from_y * 2, 2)])
        half[rows, :] = jnp.dot(block, virt[...], preferred_element_type=F32).astype(BF16)

    def offset(i):
        t = i % 4
        return t, (t + i // 16 % 4) % 4, (t + i // 4) % 4

    for dk in range(2):
        to_k = (k + dk) % 2
        done = jnp.dot(flat(gath[1, :, to_k]), half[...], preferred_element_type=F32)
        full[dk] = done.astype(BF16).reshape(4, COLS, SUB, N)

        @pl.loop(0, DEVICES // 2)
        def _(i):
            dx, dy, dz = offset(i)
            to_y, to_col = (y + dy) % 4, (x + dx) % 4 * 4 + (z + dz) % 4
            slot = dk * (DEVICES // 2) + i
            piece, arrived = full.at[dk, to_y, to_col], full_recv.at[slot // (NP // GROUPS)]

            def far():
                send(piece, full_k.at[slot], full_send, arrived, to_y * 2 + to_k, to_col)

            if dk:
                far()
            else:
                pl.when(i > 0)(far)

                @pl.when(i == 0)
                def _():
                    pltpu.make_async_copy(piece, full_k.at[0], arrived).start()

    wait(bk, col_recv)
    for row in range(ROWS):
        right[pl.ds(row * TILE, TILE), :] = flat(bk[pl.ds(row * COLS, COLS)])
    row_id = lax.broadcasted_iota(jnp.int32, (SUB, N), 0)
    col_id = lax.broadcasted_iota(jnp.int32, (SUB, N), 1)
    same = (row_id == col_id % SUB)[None]
    pick = lax.broadcasted_iota(jnp.int32, (N, NP), 0) // SUB
    pick = (pick == lax.broadcasted_iota(jnp.int32, (N, NP), 1)).astype(F32)
    size = NP // GROUPS
    for g in range(GROUPS):
        slots = pl.ds(g * size, size)
        wait(full_k.at[slots], full_recv.at[g])
        cross = lax.dot_general(
            flat(full_k[slots]), right[...], (((1,), (1,)), ((), ())), preferred_element_type=F32
        )
        kept = jnp.sum(jnp.where(same, cross.reshape(size, SUB, N), 0.0), axis=1)
        sums = jnp.dot(kept, pick, preferred_element_type=F32, precision=lax.Precision.HIGHEST)
        part[slots] = sums.reshape(size, 1, NP)

        @pl.loop(g * size, (g + 1) * size)
        def _(slot):
            dx, dy, dz = offset(slot % (DEVICES // 2))
            dk = slot // (DEVICES // 2)
            from_row = (y + 4 - dy) % 4 * 2 + (k + dk) % 2
            from_col = (x + 4 - dx) % 4 * 4 + (z + 4 - dz) % 4
            p = from_col * 8 + from_row

            @pl.when(p != me)
            def _():
                send(part.at[slot], part_in.at[me], red_send, red_recv, p // COLS, p % COLS)

            @pl.when(p == me)
            def _():
                pltpu.make_async_copy(part.at[slot], part_in.at[me], red_recv).start()

    wait(part_in, red_recv)
    out_ref[...] = jnp.sum(part_in[...], axis=0) * (-2.0 / N)

    wait(gath.at[0, :, :, 0, 0].at[pl.ds(0, 3)], ag_send.at[0])
    wait(gath.at[0, 0, 0, 0, 0], ag_send.at[0])
    wait(gath.at[0, :, :, pl.ds(0, 3), 0], ag_send.at[1])
    wait(gath.at[0, :, :, pl.ds(0, 3)], ag_send.at[2])
    wait(gath.at[0], mate_send)
    wait(bp.at[pl.ds(0, ROWS - 1)], row_send)
    wait(bk.at[pl.ds(0, 8 * (COLS - 1))], col_send)
    wait(full_k.at[pl.ds(0, DEVICES - 1)], full_send)
    wait(part_in.at[pl.ds(0, DEVICES - 1)], red_send)


def per_device(b_tensor, occ_green, virt_green, b_mask, occ_mask, virt_mask):
    hbm = pl.BlockSpec(memory_space=pltpu.HBM)
    dma = pltpu.SemaphoreType.DMA
    return pl.pallas_call(
        kernel,
        out_shape=jax.ShapeDtypeStruct((1, NP), F32),
        in_specs=[hbm] * 6,
        out_specs=pl.BlockSpec(memory_space=pltpu.VMEM),
        scratch_shapes=[
            pltpu.SMEM((8, 8), jnp.int32),
            pltpu.SMEM((8, 8), jnp.int32),
            pltpu.SMEM((8, 8), jnp.int32),
            pltpu.VMEM((8, COLS, SUB, N), BF16),
            pltpu.VMEM((2, SUB, N), BF16),
            pltpu.VMEM((2, 4, 2, 4, 4, SUB, N), BF16),
            pltpu.VMEM((ROWS, COLS, SUB, N), BF16),
            pltpu.VMEM((NP, SUB, N), BF16),
            pltpu.VMEM((N, N), BF16),
            pltpu.VMEM((N, N), BF16),
            pltpu.VMEM((2, 4, COLS, SUB, N), BF16),
            pltpu.VMEM((NP, SUB, N), BF16),
            pltpu.VMEM((N, N), BF16),
            pltpu.VMEM((NP, 1, NP), F32),
            pltpu.VMEM((DEVICES, 1, NP), F32),
            dma((5,)),
            dma((8,)),
            dma((3,)),
            dma((5,)),
            dma,
            dma,
            dma,
            dma((4,)),
            dma,
            dma,
            dma,
            dma((GROUPS,)),
            dma,
            dma,
        ],
        compiler_params=pltpu.CompilerParams(
            collective_id=0, has_side_effects=True, vmem_limit_bytes=48 * 1024 * 1024
        ),
        name="chi",
    )(b_tensor.reshape(8, COLS, SUB, N), occ_green, virt_green, b_mask, occ_mask, virt_mask)


def solution(mesh):
    return jax.shard_map(
        per_device,
        mesh=mesh,
        in_specs=(
            P("col", "row", None),
            P(("row", "col"), None),
            P(("row", "col"), None),
            P(),
            P(),
            P(),
        ),
        out_specs=P(("row", "col"), None),
        check_vma=False,
    )
```

```python
import jax
import jax.numpy as jnp
from jax import lax
from jax.experimental import pallas as pl
from jax.experimental.pallas import tpu as pltpu
from jax.sharding import PartitionSpec as P

TILE = 128
ROWS, COLS = 8, 16
DEVICES = ROWS * COLS
N = 1024
NP = 128
SUB = 8
GROUPS = 4
F32, BF16 = jnp.float32, jnp.bfloat16
rem, div = lax.rem, lax.div


def send(src, dst, send_sem, recv_sem, row, col):
    pltpu.make_async_remote_copy(
        src_ref=src,
        dst_ref=dst,
        send_sem=send_sem,
        recv_sem=recv_sem,
        device_id={"row": row, "col": col},
        device_id_type=pl.DeviceIdType.MESH,
    ).start()


def greet(sem, row, col):
    pl.semaphore_signal(
        sem, inc=1, device_id={"row": row, "col": col}, device_id_type=pl.DeviceIdType.MESH
    )


def wait(ref, sem):
    pltpu.make_async_copy(ref, ref, sem).wait()


def flat(pieces):
    return pieces.astype(F32).reshape(-1, N).astype(BF16)


def lanes(mask_ref, row):
    return jnp.concatenate(
        [jnp.full((1, TILE), mask_ref[row, j].astype(F32)) for j in range(N // TILE)], axis=1
    )


def kernel(
    b_hbm,
    occ_hbm,
    virt_hbm,
    b_mask_hbm,
    occ_mask_hbm,
    virt_mask_hbm,
    out_ref,
    b_mask,
    occ_mask,
    virt_mask,
    b,
    own,
    gath,
    bp,
    bk,
    virt,
    half,
    full,
    full_k,
    right,
    part,
    part_in,
    in_sem,
    b_sem,
    ag_send,
    ag_recv,
    line_recv,
    plane_recv,
    ready,
    mate_send,
    mate_recv,
    row_send,
    row_recv,
    col_send,
    col_recv,
    full_send,
    full_recv,
    red_send,
    red_recv,
):
    r, c = lax.axis_index("row"), lax.axis_index("col")
    y, k = div(r, 2), rem(r, 2)
    x, z = div(c, 4), rem(c, 4)
    me = r * COLS + c
    mate = r + 1 - 2 * k

    loads = [
        pltpu.make_async_copy(b_mask_hbm.at[0], b_mask, in_sem.at[0]),
        pltpu.make_async_copy(occ_mask_hbm, occ_mask, in_sem.at[1]),
        pltpu.make_async_copy(virt_mask_hbm, virt_mask, in_sem.at[2]),
        pltpu.make_async_copy(virt_hbm, own.at[0], in_sem.at[3]),
        pltpu.make_async_copy(occ_hbm, own.at[1], in_sem.at[4]),
    ]
    for load in loads:
        load.start()
    for p in range(8):
        pltpu.make_async_copy(b_hbm.at[p], b.at[p], b_sem.at[p]).start()

    barrier = pltpu.get_barrier_semaphore()
    for i in range(1, ROWS):
        greet(barrier, rem(r + i, ROWS), c)
    for i in range(1, 4):
        greet(barrier, r, rem(x + i, 4) * 4 + z)
        greet(barrier, r, x * 4 + rem(z + i, 4))

    for load in loads:
        load.wait()
    own[0] = (own[0].astype(F32) * lanes(virt_mask, r)).astype(BF16)
    own[1] = (own[1].astype(F32) * lanes(occ_mask, r)).astype(BF16)
    keep = lanes(b_mask, r)[None]

    @pl.loop(0, 8)
    def _(p):
        wait(b.at[0], b_sem.at[p])
        b[p] = (b[p].astype(F32) * keep).astype(BF16)

    pl.semaphore_wait(barrier, ROWS - 1 + 6)

    for i in range(1, 4):
        greet(ready, r, rem(x + i, 4) * 4 + z)

    a, b_at = jnp.where(k == 0, x, z), jnp.where(k == 0, z, x)

    def along_a(i):
        return jnp.where(k == 0, rem(x + i, 4) * 4 + z, x * 4 + rem(z + i, 4))

    def along_b(i):
        return jnp.where(k == 0, x * 4 + rem(z + i, 4), rem(x + i, 4) * 4 + z)

    for dk in range(2):
        to_k = rem(k + dk, 2)
        at = jnp.where(to_k == 0, x, z), jnp.where(to_k == 0, z, x)
        for dy in (0, 1, 3, 2):
            if dy + dk:
                send(
                    own.at[to_k],
                    gath.at[to_k, y, k, *at],
                    ag_send.at[0],
                    ag_recv,
                    rem(y + dy, 4) * 2 + to_k,
                    c,
                )
            else:
                pltpu.make_async_copy(own.at[k], gath.at[k, y, k, *at], ag_recv).start()

    for dk in range(2):
        for dy in (0, 1, 3, 2):
            to_row = rem(y + dy, 4) * 2 + rem(k + dk, 2)
            if dy + dk:
                send(b.at[to_row], bp.at[r], row_send, row_recv.at[dy], to_row, c)
            else:
                pltpu.make_async_copy(b.at[r], bp.at[r], row_recv.at[0]).start()

    def by_columns(*steps):
        for dx, dz in steps:
            to_col = rem(x + dx, 4) * 4 + rem(z + dz, 4)
            send(b.at[:, to_col], bk.at[pl.ds(c * 8, 8)], col_send, col_recv, r, to_col)

    pltpu.make_async_copy(b.at[:, c], bk.at[pl.ds(c * 8, 8)], col_recv).start()
    by_columns((0, 1), (1, 0), (0, 3), (3, 0))

    def line(j, q):
        return gath.at[k, :, :, rem(a + 4 - j, 4), rem(b_at + q, 4)]

    def on(ref):
        send(ref, ref, mate_send, mate_recv, mate, c)

    def spread(j):
        send(line(j, 0), line(j, 0), ag_send.at[2], plane_recv.at[3, j], r, along_b(1))
        send(line(j, 0), line(j, 0), ag_send.at[2], plane_recv.at[1, j], r, along_b(3))
        on(line(j, 0))

    def landed(j, q):
        wait(line(j, q), plane_recv.at[q, j])
        if q == 3 and j in (0, 1):
            send(line(j, q), line(j, q), ag_send.at[2], plane_recv.at[2, j], r, along_b(1))
        if q == 1 and j in (2, 3):
            send(line(j, q), line(j, q), ag_send.at[2], plane_recv.at[2, j], r, along_b(3))
        on(line(j, q))

    wait(gath.at[0, :, :, 0, 0], ag_recv)
    for j in (1, 3, 2):
        send(line(0, 0), line(0, 0), ag_send.at[1], line_recv.at[j], r, along_a(j))
    spread(0)
    pl.semaphore_wait(ready, 3)
    by_columns((0, 2), (2, 0), (1, 1), (3, 3), (1, 3), (3, 1))
    for j in (1, 3):
        wait(line(j, 0), line_recv.at[j])
        spread(j)
    landed(0, 3)
    landed(0, 1)
    wait(line(2, 0), line_recv.at[2])
    spread(2)
    by_columns((1, 2), (2, 1), (3, 2), (2, 3), (2, 2))
    for j in (1, 3, 2):
        landed(j, 3)
        landed(j, 1)
    for j in (0, 1, 3, 2):
        landed(j, 2)
    wait(gath.at[0], mate_recv)

    for row in range(ROWS):
        virt[pl.ds(row * TILE, TILE), :] = flat(gath[0, row // 2, row % 2])
    for dy in (0, 1, 3, 2):
        from_y = rem(y + 4 - dy, 4)
        wait(bp.at[pl.ds(0, 2)], row_recv.at[dy])
        rows = pl.ds(pl.multiple_of(from_y * 256, 256), 256)
        block = flat(bp[pl.ds(from_y * 2, 2)])
        half[rows, :] = jnp.dot(block, virt[...], preferred_element_type=F32).astype(BF16)

    def offset(i):
        t = rem(i, 4)
        return t, rem(t + div(i, 16) + 3, 4), rem(t + div(i, 4) + 3, 4)

    for dk in range(2):
        to_k = rem(k + dk, 2)
        done = jnp.dot(flat(gath[1, :, to_k]), half[...], preferred_element_type=F32)
        full[dk] = done.astype(BF16).reshape(4, COLS, SUB, N)

        @pl.loop(0, DEVICES // 2)
        def _(i):
            dx, dy, dz = offset(i)
            to_y, to_x, to_z = rem(y + dy, 4), rem(x + dx, 4), rem(z + dz, 4)
            slot = dk * (DEVICES // 2) + i
            piece, arrived = full.at[dk, to_y, to_z * 4 + to_x], full_recv.at[div(slot, NP // GROUPS)]

            def far():
                send(piece, full_k.at[slot], full_send, arrived, to_y * 2 + to_k, to_x * 4 + to_z)

            if dk:
                far()
            else:
                pl.when(i != 20)(far)

                @pl.when(i == 20)
                def _():
                    pltpu.make_async_copy(piece, full_k.at[20], arrived).start()

    wait(bk, col_recv)
    for row in range(ROWS):
        right[pl.ds(row * TILE, TILE), :] = flat(bk[pl.ds(row * COLS, COLS)])
    row_id = lax.broadcasted_iota(jnp.int32, (SUB, N), 0)
    col_id = lax.broadcasted_iota(jnp.int32, (SUB, N), 1)
    same = (row_id == col_id % SUB)[None]
    pick = lax.broadcasted_iota(jnp.int32, (N, NP), 0) // SUB
    pick = (pick == lax.broadcasted_iota(jnp.int32, (N, NP), 1)).astype(F32)
    size = NP // GROUPS
    for g in range(GROUPS):
        slots = pl.ds(g * size, size)
        wait(full_k.at[slots], full_recv.at[g])
        cross = lax.dot_general(
            flat(full_k[slots]), right[...], (((1,), (1,)), ((), ())), preferred_element_type=F32
        )
        kept = jnp.sum(jnp.where(same, cross.reshape(size, SUB, N), 0.0), axis=1)
        sums = jnp.dot(kept, pick, preferred_element_type=F32, precision=lax.Precision.HIGHEST)
        part[slots] = sums.reshape(size, 1, NP)

        @pl.loop(g * size, (g + 1) * size)
        def _(slot):
            dx, dy, dz = offset(rem(slot, DEVICES // 2))
            dk = (g * size) // (DEVICES // 2)
            from_row = rem(y + 4 - dy, 4) * 2 + rem(k + dk, 2)
            from_col = rem(x + 4 - dx, 4) * 4 + rem(z + 4 - dz, 4)
            p = from_col * 8 + from_row

            @pl.when(p != me)
            def _():
                send(part.at[slot], part_in.at[me], red_send, red_recv, div(p, COLS), rem(p, COLS))

            @pl.when(p == me)
            def _():
                pltpu.make_async_copy(part.at[slot], part_in.at[me], red_recv).start()

    wait(part_in, red_recv)
    out_ref[...] = jnp.sum(part_in[...], axis=0) * (-2.0 / N)

    wait(own.at[0], ag_send.at[0])
    wait(gath.at[0, pl.ds(0, 3), :, 0, 0], ag_send.at[0])
    wait(gath.at[0, :, :, pl.ds(0, 3), 0], ag_send.at[1])
    wait(gath.at[0, :, :, pl.ds(0, 3)], ag_send.at[2])
    wait(gath.at[0], mate_send)
    wait(bp.at[pl.ds(0, ROWS - 1)], row_send)
    wait(bk.at[pl.ds(0, 8 * (COLS - 1))], col_send)
    wait(full_k.at[pl.ds(0, DEVICES - 1)], full_send)
    wait(part_in.at[pl.ds(0, DEVICES - 1)], red_send)


def per_device(b_tensor, occ_green, virt_green, b_mask, occ_mask, virt_mask):
    hbm = pl.BlockSpec(memory_space=pltpu.HBM)
    dma = pltpu.SemaphoreType.DMA
    return pl.pallas_call(
        kernel,
        out_shape=jax.ShapeDtypeStruct((1, NP), F32),
        in_specs=[hbm] * 6,
        out_specs=pl.BlockSpec(memory_space=pltpu.VMEM),
        scratch_shapes=[
            pltpu.SMEM((8, 8), jnp.int32),
            pltpu.SMEM((8, 8), jnp.int32),
            pltpu.SMEM((8, 8), jnp.int32),
            pltpu.VMEM((8, COLS, SUB, N), BF16),
            pltpu.VMEM((2, SUB, N), BF16),
            pltpu.VMEM((2, 4, 2, 4, 4, SUB, N), BF16),
            pltpu.VMEM((ROWS, COLS, SUB, N), BF16),
            pltpu.VMEM((NP, SUB, N), BF16),
            pltpu.VMEM((N, N), BF16),
            pltpu.VMEM((N, N), BF16),
            pltpu.VMEM((2, 4, COLS, SUB, N), BF16),
            pltpu.VMEM((NP, SUB, N), BF16),
            pltpu.VMEM((N, N), BF16),
            pltpu.VMEM((NP, 1, NP), F32),
            pltpu.VMEM((DEVICES, 1, NP), F32),
            dma((5,)),
            dma((8,)),
            dma((3,)),
            dma,
            dma((4,)),
            dma((4, 4)),
            pltpu.SemaphoreType.REGULAR,
            dma,
            dma,
            dma,
            dma((4,)),
            dma,
            dma,
            dma,
            dma((GROUPS,)),
            dma,
            dma,
        ],
        compiler_params=pltpu.CompilerParams(
            collective_id=0, has_side_effects=True, vmem_limit_bytes=64 * 1024 * 1024 - 65536
        ),
        name="chi",
    )(b_tensor.reshape(8, COLS, SUB, N), occ_green, virt_green, b_mask, occ_mask, virt_mask)


def solution(mesh):
    return jax.shard_map(
        per_device,
        mesh=mesh,
        in_specs=(
            P("col", "row", None),
            P(("row", "col"), None),
            P(("row", "col"), None),
            P(),
            P(),
            P(),
        ),
        out_specs=P(("row", "col"), None),
        check_vma=False,
    )
```

```python
import jax
import jax.numpy as jnp
from jax import lax
from jax.experimental import pallas as pl
from jax.experimental.pallas import tpu as pltpu
from jax.sharding import PartitionSpec as P

TILE = 128
ROWS, COLS = 8, 16
DEVICES = ROWS * COLS
N = 1024
NP = 128
SUB = 8
GROUPS = 4
F32, BF16 = jnp.float32, jnp.bfloat16
rem, div = lax.rem, lax.div


def send(src, dst, send_sem, recv_sem, row, col):
    pltpu.make_async_remote_copy(
        src_ref=src,
        dst_ref=dst,
        send_sem=send_sem,
        recv_sem=recv_sem,
        device_id={"row": row, "col": col},
        device_id_type=pl.DeviceIdType.MESH,
    ).start()


def greet(sem, row, col):
    pl.semaphore_signal(
        sem, inc=1, device_id={"row": row, "col": col}, device_id_type=pl.DeviceIdType.MESH
    )


def wait(ref, sem):
    pltpu.make_async_copy(ref, ref, sem).wait()


def flat(pieces):
    return pieces.astype(F32).reshape(-1, N).astype(BF16)


def lanes(mask_ref, row):
    return jnp.concatenate(
        [jnp.full((1, TILE), mask_ref[row, j].astype(F32)) for j in range(N // TILE)], axis=1
    )


def kernel(
    b_hbm,
    occ_hbm,
    virt_hbm,
    b_mask_hbm,
    occ_mask_hbm,
    virt_mask_hbm,
    out_ref,
    b_mask,
    occ_mask,
    virt_mask,
    b,
    own,
    gath,
    bp,
    bk,
    virt,
    half,
    full,
    full_k,
    right,
    part,
    part_in,
    in_sem,
    b_sem,
    ag_send,
    ag_recv,
    line_recv,
    plane_recv,
    ready,
    mate_send,
    mate_recv,
    row_send,
    row_recv,
    col_send,
    col_recv,
    full_send,
    full_recv,
    red_send,
    red_recv,
):
    r, c = lax.axis_index("row"), lax.axis_index("col")
    y, k = div(r, 2), rem(r, 2)
    x, z = div(c, 4), rem(c, 4)
    me = r * COLS + c
    mate = r + 1 - 2 * k

    loads = [
        pltpu.make_async_copy(b_mask_hbm.at[0], b_mask, in_sem.at[0]),
        pltpu.make_async_copy(occ_mask_hbm, occ_mask, in_sem.at[1]),
        pltpu.make_async_copy(virt_mask_hbm, virt_mask, in_sem.at[2]),
        pltpu.make_async_copy(virt_hbm, own.at[0], in_sem.at[3]),
        pltpu.make_async_copy(occ_hbm, own.at[1], in_sem.at[4]),
    ]
    for load in loads:
        load.start()
    for p in range(8):
        pltpu.make_async_copy(b_hbm.at[p], b.at[p], b_sem.at[p]).start()

    barrier = pltpu.get_barrier_semaphore()
    for i in range(1, ROWS):
        greet(barrier, rem(r + i, ROWS), c)
    for i in range(1, 4):
        greet(barrier, r, rem(x + i, 4) * 4 + z)
        greet(barrier, r, x * 4 + rem(z + i, 4))

    for load in loads:
        load.wait()
    own[0] = (own[0].astype(F32) * lanes(virt_mask, r)).astype(BF16)
    own[1] = (own[1].astype(F32) * lanes(occ_mask, r)).astype(BF16)
    keep = lanes(b_mask, r)[None]

    @pl.loop(0, 8)
    def _(p):
        wait(b.at[0], b_sem.at[p])
        b[p] = (b[p].astype(F32) * keep).astype(BF16)

    pl.semaphore_wait(barrier, ROWS - 1 + 6)

    for i in range(1, 4):
        greet(ready, r, rem(x + i, 4) * 4 + z)

    a, b_at = jnp.where(k == 0, x, z), jnp.where(k == 0, z, x)

    def along_a(i):
        return jnp.where(k == 0, rem(x + i, 4) * 4 + z, x * 4 + rem(z + i, 4))

    def along_b(i):
        return jnp.where(k == 0, x * 4 + rem(z + i, 4), rem(x + i, 4) * 4 + z)

    for dk in range(2):
        to_k = rem(k + dk, 2)
        at = jnp.where(to_k == 0, z, x), jnp.where(to_k == 0, x, z)
        for dy in (0, 1, 3, 2):
            if dy + dk:
                send(
                    own.at[to_k],
                    gath.at[to_k, *at, y, k],
                    ag_send.at[0],
                    ag_recv,
                    rem(y + dy, 4) * 2 + to_k,
                    c,
                )
            else:
                pltpu.make_async_copy(own.at[k], gath.at[k, *at, y, k], ag_recv).start()

    for dk in range(2):
        for dy in (0, 1, 3, 2):
            to_row = rem(y + dy, 4) * 2 + rem(k + dk, 2)
            if dy + dk:
                send(b.at[to_row], bp.at[r], row_send, row_recv.at[dy], to_row, c)
            else:
                pltpu.make_async_copy(b.at[r], bp.at[r], row_recv.at[0]).start()

    def by_columns(*steps):
        for dx, dz in steps:
            to_col = rem(x + dx, 4) * 4 + rem(z + dz, 4)
            send(b.at[:, to_col], bk.at[pl.ds(c * 8, 8)], col_send, col_recv, r, to_col)

    pltpu.make_async_copy(b.at[:, c], bk.at[pl.ds(c * 8, 8)], col_recv).start()
    by_columns((0, 1), (1, 0), (0, 3), (3, 0), (0, 2), (2, 0))

    def line(j, q):
        return gath.at[k, rem(b_at + q, 4), rem(a + 4 - j, 4)]

    def on(ref):
        send(ref, ref, mate_send, mate_recv, mate, c)

    def spread(j):
        send(line(j, 0), line(j, 0), ag_send.at[2], plane_recv.at[3, j], r, along_b(1))
        send(line(j, 0), line(j, 0), ag_send.at[2], plane_recv.at[1, j], r, along_b(3))
        on(line(j, 0))

    def landed(j, q):
        wait(line(j, q), plane_recv.at[q, j])
        if q == 3 and j in (0, 1):
            send(line(j, q), line(j, q), ag_send.at[2], plane_recv.at[2, j], r, along_b(1))
        if q == 1 and j in (2, 3):
            send(line(j, q), line(j, q), ag_send.at[2], plane_recv.at[2, j], r, along_b(3))
        on(line(j, q))

    wait(gath.at[0, 0, 0], ag_recv)
    for j in (1, 3, 2):
        send(line(0, 0), line(0, 0), ag_send.at[1], line_recv.at[j], r, along_a(j))
    spread(0)
    pl.semaphore_wait(ready, 3)
    by_columns((1, 1), (3, 3), (1, 3), (3, 1))
    for j in (1, 3):
        wait(line(j, 0), line_recv.at[j])
        spread(j)
    landed(0, 3)
    landed(0, 1)
    wait(line(2, 0), line_recv.at[2])
    spread(2)
    by_columns((1, 2), (3, 2))
    for j in (1, 3, 2):
        landed(j, 3)
        landed(j, 1)
    for j in (0, 1, 3, 2):
        landed(j, 2)
    by_columns((2, 1), (2, 3), (2, 2))
    wait(gath.at[0], mate_recv)

    for row in range(ROWS):
        virt[pl.ds(row * TILE, TILE), :] = flat(jnp.swapaxes(gath[0, :, :, row // 2, row % 2], 0, 1))
    for dy in (0, 1, 3, 2):
        from_y = rem(y + 4 - dy, 4)
        wait(bp.at[pl.ds(0, 2)], row_recv.at[dy])
        rows = pl.ds(pl.multiple_of(from_y * 256, 256), 256)
        block = flat(bp[pl.ds(from_y * 2, 2)])
        half[rows, :] = jnp.dot(block, virt[...], preferred_element_type=F32).astype(BF16)

    def offset(i):
        t = rem(i, 4)
        return t, rem(t + div(i, 16) + 3, 4), rem(t + div(i, 4) + 3, 4)

    for dk in range(2):
        to_k = rem(k + dk, 2)
        done = jnp.dot(flat(gath[1, :, :, :, to_k]), half[...], preferred_element_type=F32)
        full[dk] = done.astype(BF16).reshape(COLS, 4, SUB, N)

    wait(bk, col_recv)
    for row in range(ROWS):
        right[pl.ds(row * TILE, TILE), :] = flat(bk[pl.ds(row * COLS, COLS)])
    for dk in range(2):
        to_k = rem(k + dk, 2)

        @pl.loop(0, DEVICES // 2)
        def _(i):
            dx, dy, dz = offset(i)
            to_y, to_x, to_z = rem(y + dy, 4), rem(x + dx, 4), rem(z + dz, 4)
            slot = dk * (DEVICES // 2) + i
            piece, arrived = full.at[dk, to_x * 4 + to_z, to_y], full_recv.at[div(slot, NP // GROUPS)]

            def far():
                send(piece, full_k.at[slot], full_send, arrived, to_y * 2 + to_k, to_x * 4 + to_z)

            if dk:
                far()
            else:
                pl.when(i != 20)(far)

                @pl.when(i == 20)
                def _():
                    pltpu.make_async_copy(piece, full_k.at[20], arrived).start()

    row_id = lax.broadcasted_iota(jnp.int32, (SUB, N), 0)
    col_id = lax.broadcasted_iota(jnp.int32, (SUB, N), 1)
    same = (row_id == col_id % SUB)[None]
    pick = lax.broadcasted_iota(jnp.int32, (N, NP), 0) // SUB
    pick = (pick == lax.broadcasted_iota(jnp.int32, (N, NP), 1)).astype(F32)
    size = NP // GROUPS
    for g in range(GROUPS):
        slots = pl.ds(g * size, size)
        wait(full_k.at[slots], full_recv.at[g])
        cross = lax.dot_general(
            flat(full_k[slots]), right[...], (((1,), (1,)), ((), ())), preferred_element_type=F32
        )
        kept = jnp.sum(jnp.where(same, cross.reshape(size, SUB, N), 0.0), axis=1)
        sums = jnp.dot(kept, pick, preferred_element_type=F32, precision=lax.Precision.HIGHEST)
        part[slots] = sums.reshape(size, 1, NP)

        @pl.loop(g * size, (g + 1) * size)
        def _(slot):
            dx, dy, dz = offset(rem(slot, DEVICES // 2))
            dk = (g * size) // (DEVICES // 2)
            from_row = rem(y + 4 - dy, 4) * 2 + rem(k + dk, 2)
            from_col = rem(x + 4 - dx, 4) * 4 + rem(z + 4 - dz, 4)
            p = from_col * 8 + from_row

            @pl.when(p != me)
            def _():
                send(part.at[slot], part_in.at[me], red_send, red_recv, div(p, COLS), rem(p, COLS))

            @pl.when(p == me)
            def _():
                pltpu.make_async_copy(part.at[slot], part_in.at[me], red_recv).start()

    wait(part_in, red_recv)
    out_ref[...] = jnp.sum(part_in[...], axis=0) * (-2.0 / N)

    wait(own.at[0], ag_send.at[0])
    wait(gath.at[0, 0, 0, pl.ds(0, 3)], ag_send.at[0])
    wait(gath.at[0, 0, pl.ds(0, 3)], ag_send.at[1])
    wait(gath.at[0, pl.ds(0, 3)], ag_send.at[2])
    wait(gath.at[0], mate_send)
    wait(bp.at[pl.ds(0, ROWS - 1)], row_send)
    wait(bk.at[pl.ds(0, 8 * (COLS - 1))], col_send)
    wait(full_k.at[pl.ds(0, DEVICES - 1)], full_send)
    wait(part_in.at[pl.ds(0, DEVICES - 1)], red_send)


def per_device(b_tensor, occ_green, virt_green, b_mask, occ_mask, virt_mask):
    hbm = pl.BlockSpec(memory_space=pltpu.HBM)
    dma = pltpu.SemaphoreType.DMA
    return pl.pallas_call(
        kernel,
        out_shape=jax.ShapeDtypeStruct((1, NP), F32),
        in_specs=[hbm] * 6,
        out_specs=pl.BlockSpec(memory_space=pltpu.VMEM),
        scratch_shapes=[
            pltpu.SMEM((8, 8), jnp.int32),
            pltpu.SMEM((8, 8), jnp.int32),
            pltpu.SMEM((8, 8), jnp.int32),
            pltpu.VMEM((8, COLS, SUB, N), BF16),
            pltpu.VMEM((2, SUB, N), BF16),
            pltpu.VMEM((2, 4, 4, 4, 2, SUB, N), BF16),
            pltpu.VMEM((ROWS, COLS, SUB, N), BF16),
            pltpu.VMEM((NP, SUB, N), BF16),
            pltpu.VMEM((N, N), BF16),
            pltpu.VMEM((N, N), BF16),
            pltpu.VMEM((2, COLS, 4, SUB, N), BF16),
            pltpu.VMEM((NP, SUB, N), BF16),
            pltpu.VMEM((N, N), BF16),
            pltpu.VMEM((NP, 1, NP), F32),
            pltpu.VMEM((DEVICES, 1, NP), F32),
            dma((5,)),
            dma((8,)),
            dma((3,)),
            dma,
            dma((4,)),
            dma((4, 4)),
            pltpu.SemaphoreType.REGULAR,
            dma,
            dma,
            dma,
            dma((4,)),
            dma,
            dma,
            dma,
            dma((GROUPS,)),
            dma,
            dma,
        ],
        compiler_params=pltpu.CompilerParams(
            collective_id=0, has_side_effects=True, vmem_limit_bytes=64 * 1024 * 1024 - 65536
        ),
        name="chi",
    )(b_tensor.reshape(8, COLS, SUB, N), occ_green, virt_green, b_mask, occ_mask, virt_mask)


def solution(mesh):
    return jax.shard_map(
        per_device,
        mesh=mesh,
        in_specs=(
            P("col", "row", None),
            P(("row", "col"), None),
            P(("row", "col"), None),
            P(),
            P(),
            P(),
        ),
        out_specs=P(("row", "col"), None),
        check_vma=False,
    )
```

```python
import jax
import jax.numpy as jnp
from jax import lax
from jax.experimental import pallas as pl
from jax.experimental.pallas import tpu as pltpu
from jax.sharding import PartitionSpec as P

TILE = 128
ROWS, COLS = 8, 16
DEVICES = ROWS * COLS
N = 1024
NP = 128
SUB = 8
GROUPS = 4
F32, BF16 = jnp.float32, jnp.bfloat16
rem, div = lax.rem, lax.div


def send(src, dst, send_sem, recv_sem, row, col):
    pltpu.make_async_remote_copy(
        src_ref=src,
        dst_ref=dst,
        send_sem=send_sem,
        recv_sem=recv_sem,
        device_id={"row": row, "col": col},
        device_id_type=pl.DeviceIdType.MESH,
    ).start()


def greet(sem, row, col):
    pl.semaphore_signal(
        sem, inc=1, device_id={"row": row, "col": col}, device_id_type=pl.DeviceIdType.MESH
    )


def wait(ref, sem):
    pltpu.make_async_copy(ref, ref, sem).wait()


def flat(pieces):
    return pieces.astype(F32).reshape(-1, N).astype(BF16)


def lanes(mask_ref, row):
    return jnp.concatenate(
        [jnp.full((1, TILE), mask_ref[row, j].astype(F32)) for j in range(N // TILE)], axis=1
    )


def kernel(
    b_hbm,
    occ_hbm,
    virt_hbm,
    b_mask_hbm,
    occ_mask_hbm,
    virt_mask_hbm,
    out_ref,
    b_mask,
    occ_mask,
    virt_mask,
    b,
    own,
    gath,
    bp,
    bk,
    virt,
    half,
    full,
    full_k,
    right,
    part,
    part_in,
    in_sem,
    b_sem,
    ag_send,
    ag_recv,
    line_recv,
    plane_recv,
    ready,
    mate_send,
    mate_recv,
    row_send,
    row_recv,
    col_send,
    col_recv,
    full_send,
    full_recv,
    red_send,
    red_recv,
):
    r, c = lax.axis_index("row"), lax.axis_index("col")
    y, k = div(r, 2), rem(r, 2)
    x, z = div(c, 4), rem(c, 4)
    me = r * COLS + c
    mate = r + 1 - 2 * k

    loads = [
        pltpu.make_async_copy(b_mask_hbm.at[0], b_mask, in_sem.at[0]),
        pltpu.make_async_copy(occ_mask_hbm, occ_mask, in_sem.at[1]),
        pltpu.make_async_copy(virt_mask_hbm, virt_mask, in_sem.at[2]),
        pltpu.make_async_copy(virt_hbm, own.at[0], in_sem.at[3]),
        pltpu.make_async_copy(occ_hbm, own.at[1], in_sem.at[4]),
    ]
    for load in loads:
        load.start()
    for p in range(8):
        pltpu.make_async_copy(b_hbm.at[p], b.at[p], b_sem.at[p]).start()

    barrier = pltpu.get_barrier_semaphore()
    for i in range(1, ROWS):
        greet(barrier, rem(r + i, ROWS), c)
    for i in range(1, 4):
        greet(barrier, r, rem(x + i, 4) * 4 + z)
        greet(barrier, r, x * 4 + rem(z + i, 4))

    for load in loads:
        load.wait()
    own[0] = (own[0].astype(F32) * lanes(virt_mask, r)).astype(BF16)
    own[1] = (own[1].astype(F32) * lanes(occ_mask, r)).astype(BF16)
    keep = lanes(b_mask, r)[None]

    @pl.loop(0, 8)
    def _(p):
        wait(b.at[0], b_sem.at[p])
        b[p] = (b[p].astype(F32) * keep).astype(BF16)

    pl.semaphore_wait(barrier, ROWS - 1 + 6)

    for i in range(1, 4):
        greet(ready, r, rem(x + i, 4) * 4 + z)

    a, b_at = jnp.where(k == 0, x, z), jnp.where(k == 0, z, x)

    def along_a(i):
        return jnp.where(k == 0, rem(x + i, 4) * 4 + z, x * 4 + rem(z + i, 4))

    def along_b(i):
        return jnp.where(k == 0, x * 4 + rem(z + i, 4), rem(x + i, 4) * 4 + z)

    for dk in range(2):
        to_k = rem(k + dk, 2)
        at = jnp.where(to_k == 0, z, x), jnp.where(to_k == 0, x, z)
        for dy in (0, 1, 3, 2):
            if dy + dk:
                send(
                    own.at[to_k],
                    gath.at[to_k, *at, y, k],
                    ag_send.at[0],
                    ag_recv,
                    rem(y + dy, 4) * 2 + to_k,
                    c,
                )
            else:
                pltpu.make_async_copy(own.at[k], gath.at[k, *at, y, k], ag_recv).start()

    for dk in range(2):
        for dy in (0, 1, 3, 2):
            to_row = rem(y + dy, 4) * 2 + rem(k + dk, 2)
            if dy + dk:
                send(b.at[to_row], bp.at[r], row_send, row_recv.at[dy], to_row, c)
            else:
                pltpu.make_async_copy(b.at[r], bp.at[r], row_recv.at[0]).start()

    def by_columns(*steps):
        for dx, dz in steps:
            to_col = rem(x + dx, 4) * 4 + rem(z + dz, 4)
            send(b.at[:, to_col], bk.at[pl.ds(c * 8, 8)], col_send, col_recv, r, to_col)

    pltpu.make_async_copy(b.at[:, c], bk.at[pl.ds(c * 8, 8)], col_recv).start()
    by_columns((0, 1), (1, 0), (0, 3), (3, 0), (0, 2), (2, 0))

    def line(j, q):
        return gath.at[k, rem(b_at + q, 4), rem(a + 4 - j, 4)]

    def on(ref):
        send(ref, ref, mate_send, mate_recv, mate, c)

    def spread(j):
        send(line(j, 0), line(j, 0), ag_send.at[2], plane_recv.at[3, j], r, along_b(1))
        send(line(j, 0), line(j, 0), ag_send.at[2], plane_recv.at[1, j], r, along_b(3))
        on(line(j, 0))

    def landed(j, q):
        wait(line(j, q), plane_recv.at[q, j])
        if q == 3 and j in (0, 1):
            send(line(j, q), line(j, q), ag_send.at[2], plane_recv.at[2, j], r, along_b(1))
        if q == 1 and j in (2, 3):
            send(line(j, q), line(j, q), ag_send.at[2], plane_recv.at[2, j], r, along_b(3))
        on(line(j, q))

    wait(gath.at[0, 0, 0], ag_recv)
    for j in (1, 3, 2):
        send(line(0, 0), line(0, 0), ag_send.at[1], line_recv.at[j], r, along_a(j))
    spread(0)
    pl.semaphore_wait(ready, 3)
    by_columns((1, 1), (3, 3), (1, 3), (3, 1))
    for j in (1, 3):
        wait(line(j, 0), line_recv.at[j])
        spread(j)
    landed(0, 3)
    by_columns((1, 2), (3, 2))
    landed(0, 1)
    wait(line(2, 0), line_recv.at[2])
    spread(2)
    for j in (1, 3, 2):
        landed(j, 3)
        landed(j, 1)
    for j in (0, 1, 3, 2):
        landed(j, 2)
    by_columns((2, 1), (2, 3), (2, 2))
    wait(gath.at[0], mate_recv)

    for row in range(ROWS):
        virt[pl.ds(row * TILE, TILE), :] = flat(jnp.swapaxes(gath[0, :, :, row // 2, row % 2], 0, 1))
    for dy in (0, 1, 3, 2):
        from_y = rem(y + 4 - dy, 4)
        wait(bp.at[pl.ds(0, 2)], row_recv.at[dy])
        rows = pl.ds(pl.multiple_of(from_y * 256, 256), 256)
        block = flat(bp[pl.ds(from_y * 2, 2)])
        half[rows, :] = jnp.dot(block, virt[...], preferred_element_type=F32).astype(BF16)

    def offset(i):
        t = rem(i, 4)
        return t, rem(t + div(i, 16) + 3, 4), rem(t + div(i, 4) + 3, 4)

    for dk in range(2):
        to_k = rem(k + dk, 2)
        done = jnp.dot(flat(gath[1, :, :, :, to_k]), half[...], preferred_element_type=F32)
        full[dk] = done.astype(BF16).reshape(COLS, 4, SUB, N)

    wait(bk, col_recv)
    for row in range(ROWS):
        right[pl.ds(row * TILE, TILE), :] = flat(bk[pl.ds(row * COLS, COLS)])
    for dk in range(2):
        to_k = rem(k + dk, 2)

        @pl.loop(0, DEVICES // 2)
        def _(i):
            dx, dy, dz = offset(i)
            to_y, to_x, to_z = rem(y + dy, 4), rem(x + dx, 4), rem(z + dz, 4)
            slot = dk * (DEVICES // 2) + i
            piece, arrived = full.at[dk, to_x * 4 + to_z, to_y], full_recv.at[div(slot, NP // GROUPS)]

            def far():
                send(piece, full_k.at[slot], full_send, arrived, to_y * 2 + to_k, to_x * 4 + to_z)

            if dk:
                far()
            else:
                pl.when(i != 20)(far)

                @pl.when(i == 20)
                def _():
                    pltpu.make_async_copy(piece, full_k.at[20], arrived).start()

    row_id = lax.broadcasted_iota(jnp.int32, (SUB, N), 0)
    col_id = lax.broadcasted_iota(jnp.int32, (SUB, N), 1)
    same = (row_id == col_id % SUB)[None]
    pick = lax.broadcasted_iota(jnp.int32, (N, NP), 0) // SUB
    pick = (pick == lax.broadcasted_iota(jnp.int32, (N, NP), 1)).astype(F32)
    size = NP // GROUPS
    for g in range(GROUPS):
        slots = pl.ds(g * size, size)
        wait(full_k.at[slots], full_recv.at[g])
        cross = lax.dot_general(
            flat(full_k[slots]), right[...], (((1,), (1,)), ((), ())), preferred_element_type=F32
        )
        kept = jnp.sum(jnp.where(same, cross.reshape(size, SUB, N), 0.0), axis=1)
        sums = jnp.dot(kept, pick, preferred_element_type=F32, precision=lax.Precision.HIGHEST)
        part[slots] = sums.reshape(size, 1, NP)

        @pl.loop(g * size, (g + 1) * size)
        def _(slot):
            dx, dy, dz = offset(rem(slot, DEVICES // 2))
            dk = (g * size) // (DEVICES // 2)
            from_row = rem(y + 4 - dy, 4) * 2 + rem(k + dk, 2)
            from_col = rem(x + 4 - dx, 4) * 4 + rem(z + 4 - dz, 4)
            p = from_col * 8 + from_row

            @pl.when(p != me)
            def _():
                send(part.at[slot], part_in.at[me], red_send, red_recv, div(p, COLS), rem(p, COLS))

            @pl.when(p == me)
            def _():
                pltpu.make_async_copy(part.at[slot], part_in.at[me], red_recv).start()

    wait(part_in, red_recv)
    out_ref[...] = jnp.sum(part_in[...], axis=0) * (-2.0 / N)

    wait(own.at[0], ag_send.at[0])
    wait(gath.at[0, 0, 0, pl.ds(0, 3)], ag_send.at[0])
    wait(gath.at[0, 0, pl.ds(0, 3)], ag_send.at[1])
    wait(gath.at[0, pl.ds(0, 3)], ag_send.at[2])
    wait(gath.at[0], mate_send)
    wait(bp.at[pl.ds(0, ROWS - 1)], row_send)
    wait(bk.at[pl.ds(0, 8 * (COLS - 1))], col_send)
    wait(full_k.at[pl.ds(0, DEVICES - 1)], full_send)
    wait(part_in.at[pl.ds(0, DEVICES - 1)], red_send)


def per_device(b_tensor, occ_green, virt_green, b_mask, occ_mask, virt_mask):
    hbm = pl.BlockSpec(memory_space=pltpu.HBM)
    dma = pltpu.SemaphoreType.DMA
    return pl.pallas_call(
        kernel,
        out_shape=jax.ShapeDtypeStruct((1, NP), F32),
        in_specs=[hbm] * 6,
        out_specs=pl.BlockSpec(memory_space=pltpu.VMEM),
        scratch_shapes=[
            pltpu.SMEM((8, 8), jnp.int32),
            pltpu.SMEM((8, 8), jnp.int32),
            pltpu.SMEM((8, 8), jnp.int32),
            pltpu.VMEM((8, COLS, SUB, N), BF16),
            pltpu.VMEM((2, SUB, N), BF16),
            pltpu.VMEM((2, 4, 4, 4, 2, SUB, N), BF16),
            pltpu.VMEM((ROWS, COLS, SUB, N), BF16),
            pltpu.VMEM((NP, SUB, N), BF16),
            pltpu.VMEM((N, N), BF16),
            pltpu.VMEM((N, N), BF16),
            pltpu.VMEM((2, COLS, 4, SUB, N), BF16),
            pltpu.VMEM((NP, SUB, N), BF16),
            pltpu.VMEM((N, N), BF16),
            pltpu.VMEM((NP, 1, NP), F32),
            pltpu.VMEM((DEVICES, 1, NP), F32),
            dma((5,)),
            dma((8,)),
            dma((3,)),
            dma,
            dma((4,)),
            dma((4, 4)),
            pltpu.SemaphoreType.REGULAR,
            dma,
            dma,
            dma,
            dma((4,)),
            dma,
            dma,
            dma,
            dma((GROUPS,)),
            dma,
            dma,
        ],
        compiler_params=pltpu.CompilerParams(
            collective_id=0, has_side_effects=True, vmem_limit_bytes=64 * 1024 * 1024 - 65536
        ),
        name="chi",
    )(b_tensor.reshape(8, COLS, SUB, N), occ_green, virt_green, b_mask, occ_mask, virt_mask)


def solution(mesh):
    return jax.shard_map(
        per_device,
        mesh=mesh,
        in_specs=(
            P("col", "row", None),
            P(("row", "col"), None),
            P(("row", "col"), None),
            P(),
            P(),
            P(),
        ),
        out_specs=P(("row", "col"), None),
        check_vma=False,
    )
```

```python
import jax
import jax.numpy as jnp
from jax import lax
from jax.experimental import pallas as pl
from jax.experimental.pallas import tpu as pltpu
from jax.sharding import PartitionSpec as P

TILE = 128
ROWS, COLS = 8, 16
DEVICES = ROWS * COLS
N = 1024
NP = 128
SUB = 8
GROUPS = 4
F32, BF16 = jnp.float32, jnp.bfloat16
rem, div = lax.rem, lax.div


def send(src, dst, send_sem, recv_sem, row, col):
    pltpu.make_async_remote_copy(
        src_ref=src,
        dst_ref=dst,
        send_sem=send_sem,
        recv_sem=recv_sem,
        device_id={"row": row, "col": col},
        device_id_type=pl.DeviceIdType.MESH,
    ).start()


def greet(sem, row, col):
    pl.semaphore_signal(
        sem, inc=1, device_id={"row": row, "col": col}, device_id_type=pl.DeviceIdType.MESH
    )


def wait(ref, sem):
    pltpu.make_async_copy(ref, ref, sem).wait()


def flat(pieces):
    return pieces.astype(F32).reshape(-1, N).astype(BF16)


def lanes(mask_ref, row):
    return jnp.concatenate(
        [jnp.full((1, TILE), mask_ref[row, j].astype(F32)) for j in range(N // TILE)], axis=1
    )


def kernel(
    b_hbm,
    occ_hbm,
    virt_hbm,
    b_mask_hbm,
    occ_mask_hbm,
    virt_mask_hbm,
    out_ref,
    b_mask,
    occ_mask,
    virt_mask,
    b,
    own,
    gath,
    bp,
    bk,
    virt,
    half,
    full,
    full_k,
    right,
    part,
    part_in,
    in_sem,
    b_sem,
    ag_send,
    ag_recv,
    line_recv,
    plane_recv,
    ready,
    mate_send,
    mate_recv,
    row_send,
    row_recv,
    col_send,
    col_recv,
    full_send,
    full_recv,
    red_send,
    red_recv,
):
    r, c = lax.axis_index("row"), lax.axis_index("col")
    y, k = div(r, 2), rem(r, 2)
    x, z = div(c, 4), rem(c, 4)
    me = r * COLS + c
    mate = r + 1 - 2 * k

    loads = [
        pltpu.make_async_copy(b_mask_hbm.at[0], b_mask, in_sem.at[0]),
        pltpu.make_async_copy(occ_mask_hbm, occ_mask, in_sem.at[1]),
        pltpu.make_async_copy(virt_mask_hbm, virt_mask, in_sem.at[2]),
        pltpu.make_async_copy(virt_hbm, own.at[0], in_sem.at[3]),
        pltpu.make_async_copy(occ_hbm, own.at[1], in_sem.at[4]),
    ]
    for load in loads:
        load.start()
    for p in range(8):
        pltpu.make_async_copy(b_hbm.at[p], b.at[p], b_sem.at[p]).start()

    barrier = pltpu.get_barrier_semaphore()
    for i in range(1, ROWS):
        greet(barrier, rem(r + i, ROWS), c)
    for i in range(1, 4):
        greet(barrier, r, rem(x + i, 4) * 4 + z)
        greet(barrier, r, x * 4 + rem(z + i, 4))

    for load in loads:
        load.wait()
    own[0] = (own[0].astype(F32) * lanes(virt_mask, r)).astype(BF16)
    own[1] = (own[1].astype(F32) * lanes(occ_mask, r)).astype(BF16)
    keep = lanes(b_mask, r)[None]

    @pl.loop(0, 8)
    def _(p):
        wait(b.at[0], b_sem.at[p])
        b[p] = (b[p].astype(F32) * keep).astype(BF16)

    pl.semaphore_wait(barrier, ROWS - 1 + 6)

    for i in range(1, 4):
        greet(ready, r, rem(x + i, 4) * 4 + z)

    a, b_at = jnp.where(k == 0, x, z), jnp.where(k == 0, z, x)

    def along_a(i):
        return jnp.where(k == 0, rem(x + i, 4) * 4 + z, x * 4 + rem(z + i, 4))

    def along_b(i):
        return jnp.where(k == 0, x * 4 + rem(z + i, 4), rem(x + i, 4) * 4 + z)

    for dk in range(2):
        to_k = rem(k + dk, 2)
        at = jnp.where(to_k == 0, z, x), jnp.where(to_k == 0, x, z)
        for dy in (0, 1, 3, 2):
            if dy + dk:
                send(
                    own.at[to_k],
                    gath.at[to_k, *at, y, k],
                    ag_send.at[0],
                    ag_recv,
                    rem(y + dy, 4) * 2 + to_k,
                    c,
                )
            else:
                pltpu.make_async_copy(own.at[k], gath.at[k, *at, y, k], ag_recv).start()

    for dk in range(2):
        for dy in (0, 1, 3, 2):
            to_row = rem(y + dy, 4) * 2 + rem(k + dk, 2)
            if dy + dk:
                send(b.at[to_row], bp.at[r], row_send, row_recv.at[dy], to_row, c)
            else:
                pltpu.make_async_copy(b.at[r], bp.at[r], row_recv.at[0]).start()

    def by_columns(*steps):
        for dx, dz in steps:
            to_col = rem(x + dx, 4) * 4 + rem(z + dz, 4)
            send(b.at[:, to_col], bk.at[pl.ds(c * 8, 8)], col_send, col_recv, r, to_col)

    pltpu.make_async_copy(b.at[:, c], bk.at[pl.ds(c * 8, 8)], col_recv).start()
    by_columns((0, 1), (1, 0), (0, 3), (3, 0), (0, 2), (2, 0))

    def line(j, q):
        return gath.at[k, rem(b_at + q, 4), rem(a + 4 - j, 4)]

    def on(ref):
        send(ref, ref, mate_send, mate_recv, mate, c)

    def spread(j):
        send(line(j, 0), line(j, 0), ag_send.at[2], plane_recv.at[3, j], r, along_b(1))
        send(line(j, 0), line(j, 0), ag_send.at[2], plane_recv.at[1, j], r, along_b(3))
        on(line(j, 0))

    def landed(j, q):
        wait(line(j, q), plane_recv.at[q, j])
        if q == 3 and j in (0, 1):
            send(line(j, q), line(j, q), ag_send.at[2], plane_recv.at[2, j], r, along_b(1))
        if q == 1 and j in (2, 3):
            send(line(j, q), line(j, q), ag_send.at[2], plane_recv.at[2, j], r, along_b(3))
        on(line(j, q))

    wait(gath.at[0, 0, 0], ag_recv)
    for j in (1, 3, 2):
        send(line(0, 0), line(0, 0), ag_send.at[1], line_recv.at[j], r, along_a(j))
    spread(0)
    pl.semaphore_wait(ready, 3)
    by_columns((1, 1), (3, 3), (1, 3), (3, 1))
    for j in (1, 3):
        wait(line(j, 0), line_recv.at[j])
        spread(j)
    landed(0, 3)
    by_columns((1, 2), (3, 2))
    landed(0, 1)
    wait(line(2, 0), line_recv.at[2])
    spread(2)
    for j in (1, 3, 2):
        landed(j, 3)
        landed(j, 1)
    for j in (0, 1, 3, 2):
        landed(j, 2)
    by_columns((2, 1), (2, 3), (2, 2))
    wait(gath.at[0], mate_recv)

    for row in range(ROWS):
        virt[pl.ds(row * TILE, TILE), :] = flat(jnp.swapaxes(gath[0, :, :, row // 2, row % 2], 0, 1))
    for dy in (0, 1, 3, 2):
        from_y = rem(y + 4 - dy, 4)
        wait(bp.at[pl.ds(0, 2)], row_recv.at[dy])
        rows = pl.ds(pl.multiple_of(from_y * 256, 256), 256)
        block = flat(bp[pl.ds(from_y * 2, 2)])
        half[rows, :] = jnp.dot(block, virt[...], preferred_element_type=F32).astype(BF16)

    def offset(i):
        t = rem(i, 4)
        return t, rem(t + div(i, 16) + 3, 4), rem(t + div(i, 4) + 3, 4)

    for dk in range(2):
        to_k = rem(k + dk, 2)
        done = jnp.dot(flat(gath[1, :, :, :, to_k]), half[...], preferred_element_type=F32)
        full[dk] = done.astype(BF16).reshape(COLS, 4, SUB, N)

    wait(bk, col_recv)
    for dk in range(2):
        to_k = rem(k + dk, 2)

        @pl.loop(0, DEVICES // 2)
        def _(i):
            dx, dy, dz = offset(i)
            to_y, to_x, to_z = rem(y + dy, 4), rem(x + dx, 4), rem(z + dz, 4)
            slot = dk * (DEVICES // 2) + i
            piece, arrived = full.at[dk, to_x * 4 + to_z, to_y], full_recv.at[div(slot, NP // GROUPS)]

            def far():
                send(piece, full_k.at[slot], full_send, arrived, to_y * 2 + to_k, to_x * 4 + to_z)

            if dk:
                far()
            else:
                pl.when(i != 20)(far)

                @pl.when(i == 20)
                def _():
                    pltpu.make_async_copy(piece, full_k.at[20], arrived).start()

    for row in range(ROWS):
        right[pl.ds(row * TILE, TILE), :] = flat(bk[pl.ds(row * COLS, COLS)])
    row_id = lax.broadcasted_iota(jnp.int32, (SUB, N), 0)
    col_id = lax.broadcasted_iota(jnp.int32, (SUB, N), 1)
    same = (row_id == col_id % SUB)[None]
    pick = lax.broadcasted_iota(jnp.int32, (N, NP), 0) // SUB
    pick = (pick == lax.broadcasted_iota(jnp.int32, (N, NP), 1)).astype(F32)
    size = NP // GROUPS
    for g in range(GROUPS):
        slots = pl.ds(g * size, size)
        wait(full_k.at[slots], full_recv.at[g])
        cross = lax.dot_general(
            flat(full_k[slots]), right[...], (((1,), (1,)), ((), ())), preferred_element_type=F32
        )
        kept = jnp.sum(jnp.where(same, cross.reshape(size, SUB, N), 0.0), axis=1)
        sums = jnp.dot(kept, pick, preferred_element_type=F32, precision=lax.Precision.HIGHEST)
        part[slots] = sums.reshape(size, 1, NP)

        @pl.loop(g * size, (g + 1) * size)
        def _(slot):
            dx, dy, dz = offset(rem(slot, DEVICES // 2))
            dk = (g * size) // (DEVICES // 2)
            from_row = rem(y + 4 - dy, 4) * 2 + rem(k + dk, 2)
            from_col = rem(x + 4 - dx, 4) * 4 + rem(z + 4 - dz, 4)
            p = from_col * 8 + from_row

            @pl.when(p != me)
            def _():
                send(part.at[slot], part_in.at[me], red_send, red_recv, div(p, COLS), rem(p, COLS))

            @pl.when(p == me)
            def _():
                pltpu.make_async_copy(part.at[slot], part_in.at[me], red_recv).start()

    wait(part_in, red_recv)
    out_ref[...] = jnp.sum(part_in[...], axis=0) * (-2.0 / N)

    wait(own.at[0], ag_send.at[0])
    wait(gath.at[0, 0, 0, pl.ds(0, 3)], ag_send.at[0])
    wait(gath.at[0, 0, pl.ds(0, 3)], ag_send.at[1])
    wait(gath.at[0, pl.ds(0, 3)], ag_send.at[2])
    wait(gath.at[0], mate_send)
    wait(bp.at[pl.ds(0, ROWS - 1)], row_send)
    wait(bk.at[pl.ds(0, 8 * (COLS - 1))], col_send)
    wait(full_k.at[pl.ds(0, DEVICES - 1)], full_send)
    wait(part_in.at[pl.ds(0, DEVICES - 1)], red_send)


def per_device(b_tensor, occ_green, virt_green, b_mask, occ_mask, virt_mask):
    hbm = pl.BlockSpec(memory_space=pltpu.HBM)
    dma = pltpu.SemaphoreType.DMA
    return pl.pallas_call(
        kernel,
        out_shape=jax.ShapeDtypeStruct((1, NP), F32),
        in_specs=[hbm] * 6,
        out_specs=pl.BlockSpec(memory_space=pltpu.VMEM),
        scratch_shapes=[
            pltpu.SMEM((8, 8), jnp.int32),
            pltpu.SMEM((8, 8), jnp.int32),
            pltpu.SMEM((8, 8), jnp.int32),
            pltpu.VMEM((8, COLS, SUB, N), BF16),
            pltpu.VMEM((2, SUB, N), BF16),
            pltpu.VMEM((2, 4, 4, 4, 2, SUB, N), BF16),
            pltpu.VMEM((ROWS, COLS, SUB, N), BF16),
            pltpu.VMEM((NP, SUB, N), BF16),
            pltpu.VMEM((N, N), BF16),
            pltpu.VMEM((N, N), BF16),
            pltpu.VMEM((2, COLS, 4, SUB, N), BF16),
            pltpu.VMEM((NP, SUB, N), BF16),
            pltpu.VMEM((N, N), BF16),
            pltpu.VMEM((NP, 1, NP), F32),
            pltpu.VMEM((DEVICES, 1, NP), F32),
            dma((5,)),
            dma((8,)),
            dma((3,)),
            dma,
            dma((4,)),
            dma((4, 4)),
            pltpu.SemaphoreType.REGULAR,
            dma,
            dma,
            dma,
            dma((4,)),
            dma,
            dma,
            dma,
            dma((GROUPS,)),
            dma,
            dma,
        ],
        compiler_params=pltpu.CompilerParams(
            collective_id=0, has_side_effects=True, vmem_limit_bytes=64 * 1024 * 1024 - 65536
        ),
        name="chi",
    )(b_tensor.reshape(8, COLS, SUB, N), occ_green, virt_green, b_mask, occ_mask, virt_mask)


def solution(mesh):
    return jax.shard_map(
        per_device,
        mesh=mesh,
        in_specs=(
            P("col", "row", None),
            P(("row", "col"), None),
            P(("row", "col"), None),
            P(),
            P(),
            P(),
        ),
        out_specs=P(("row", "col"), None),
        check_vma=False,
    )
```
